32 devices in a mesh: blk: 16 (over z, y, x), grp: 2 (over core).
Axes of the slice: x: 2, y: 2, z: 4, core: 2. Of those that a mesh axis runs over, the one named last changes fastest.
Arguments:
- schur_blocks: bfloat16 [64, 1024, 1024], P(('blk', 'grp')), may hold values from -1 to 5, as said below
- residual: float32 [64, 1024, 128], P(('blk', 'grp')), may hold values from -200 to 200
- direction: float32 [64, 1024, 128], P(('blk', 'grp')), may hold values from -200 to 200
- corner_map: int32 [64, 24], P(('blk', 'grp')), may hold values from 0 to 511
- panel_order: int32 [8], replicated, may hold values from 0 to 7, each once
- coarse_factor: float32 [8, 8, 1024, 1024], P(None, None, 'blk'), may hold values from -0.0625 to 0.0625
- block_inverses: float32 [8, 1024, 1024], P(None, 'blk'), may hold values from -0.1875 to 0.1875
Outputs:
- residual_next: float32 [64, 1024, 128], P(('blk', 'grp'))
- direction_next: float32 [64, 1024, 128], P(('blk', 'grp'))
The draws below stay inside these ranges and needn't reach their ends.
Inputs may be any that keep to these rules, and one draw needn't show every extreme that they name: `schur_blocks`: each subdomain's block is symmetric positive definite. `panel_order`: each coarse block appears once.
All inputs are finite; a program needn't handle non-finite values.
Results may differ from the reference program's by a relative error of at most 0.0048.
Values sent between devices are 32-bit elements; how exact they have to be, the bound alone decides.
No kernel may reach another device: no remote copies, remote signals or barrier semaphores. Data moves between devices by JAX's collectives and lax.ppermute only.
A program may use at most 64 MiB of HBM per device.

```python
import math
import jax
import jax.numpy as jnp
from jax import lax

NI = 1024
CB = 1024
PANELS = 8
COR = 24
NV = 128
SUB_DEV = 2
ITERS = 1
SUBS = 64
ROWS_B = 64
N_GRP = 2


def draw_schur_blocks(key, part):
    first_key, second_key = jax.random.split(jax.random.fold_in(key, 5))
    jitter = jax.random.normal(first_key, (SUBS, NI, NI))
    jitter = jnp.clip(jitter, -4.0, 4.0) * (0.18 / math.sqrt(NI))
    symmetric = jitter + jnp.swapaxes(jitter, 1, 2)
    diagonal = jnp.exp(jax.random.uniform(second_key, (SUBS, NI)) * math.log(4.0))
    identity = jnp.eye(NI, dtype=jnp.float32)
    return (symmetric + diagonal[:, :, None] * identity).astype(jnp.bfloat16)


def field_draw(key):
    first_key, second_key, third_key = jax.random.split(key, 3)
    growth = 3.0 ** (jnp.arange(SUBS, dtype=jnp.float32) / max(SUBS - 1, 1))
    row_scale = jnp.exp(jax.random.uniform(second_key, (SUBS, NI, 1)) * math.log(10.0))
    col_scale = jnp.exp(jax.random.uniform(third_key, (1, 1, NV)) * math.log(10.0))
    entries = jnp.clip(jax.random.normal(first_key, (SUBS, NI, NV)), -4.0, 4.0)
    return (entries * growth[:, None, None] * row_scale * col_scale / 20.0).astype(jnp.float32)


def draw_residual(key, part):
    return field_draw(jax.random.fold_in(key, 11))


def draw_direction(key, part):
    return field_draw(jax.random.fold_in(key, 23))


def set_ends(drawn, rng, least, top_value):
    index_at = [jax.random.randint(jax.random.fold_in(rng, axis), (), 0, length) for axis, length in enumerate(drawn.shape)]
    longest = drawn.shape.index(max(drawn.shape))
    neighbour = index_at[:longest] + [(index_at[longest] + 1) % drawn.shape[longest]] + index_at[longest + 1:]
    return drawn.at[tuple(index_at)].set(least).at[tuple(neighbour)].set(top_value)


def shard_levels(stream_key, dims, cuts, low, high):
    def one(axis_at, blocks):
        draws = jax.random.uniform(jax.random.fold_in(jax.random.fold_in(stream_key, 6), axis_at), (blocks,), jnp.float32, low / len(cuts), high / len(cuts))
        return jnp.repeat(jnp.exp(draws), dims[axis_at] // blocks).reshape((-1,) + (1,) * (len(dims) - axis_at - 1))

    gain = one(*cuts[0])
    for cut in cuts[1:]:
        gain = gain * one(*cut)
    return gain


def centred(key, shape, deviation, bound, cuts=(), held_as=jnp.bfloat16):
    level = shard_levels(key, shape, cuts, -0.22, 0.18) if cuts else 1.0
    values = jax.random.normal(key, shape, jnp.float32) * deviation * level
    return jnp.minimum(jnp.maximum(values, -bound), bound).astype(held_as)


def setup_inputs(seed: int = 0) -> dict:
    splits = jax.random.split(jax.random.key(seed), 8)
    schur_blocks = draw_schur_blocks(jax.random.fold_in(splits[7], 71), 0)
    residual = draw_residual(jax.random.fold_in(splits[7], 71), 0)
    direction = draw_direction(jax.random.fold_in(splits[7], 71), 0)
    corner_map = set_ends(jax.random.randint(splits[3], (SUBS, COR), 0, PANELS * ROWS_B), jax.random.fold_in(splits[3], 1), 0, (PANELS * ROWS_B) - 1).astype(jnp.int32)
    panel_order = jax.random.permutation(splits[4], PANELS).astype(jnp.int32)
    coarse_factor = centred(splits[5], (PANELS, PANELS, CB, CB), (PANELS * CB) ** -0.5, 0.0625, ((2, 16),), jnp.float32)
    block_inverses = centred(splits[6], (PANELS, CB, CB), CB ** -0.5, 0.1875, ((1, 16),), jnp.float32)
    return dict(schur_blocks=schur_blocks, residual=residual, direction=direction, corner_map=corner_map, panel_order=panel_order, coarse_factor=coarse_factor, block_inverses=block_inverses)


precise = lax.Precision.HIGHEST


def coarse_solve(coarse, panel_order, coarse_factor, block_inverses):
    solved = jnp.zeros_like(coarse)
    for position in range(PANELS):
        current = panel_order[position]
        target = coarse[current]
        for earlier in range(position):
            earlier_block = panel_order[earlier]
            target = target - jnp.dot(coarse_factor[current, earlier_block], solved[earlier_block], precision=precise)
        block_value = jnp.dot(block_inverses[current], target, precision=precise)
        solved = solved.at[current].set(block_value)
    return solved


def reference(schur_blocks, residual, direction, corner_map, panel_order, coarse_factor, block_inverses):
    sub_count = schur_blocks.shape[0]
    columns_count = residual.shape[2]
    owners = jnp.arange(sub_count, dtype=jnp.int32) // (SUB_DEV * N_GRP)
    coarse_index = (corner_map // ROWS_B) * CB + owners[:, None] * ROWS_B + corner_map % ROWS_B
    coarse_index = coarse_index.reshape(-1).astype(jnp.int32)

    def matvec(pieces):
        matrix, operand = pieces
        rounded = operand.astype(jnp.bfloat16).astype(jnp.float32)
        return jnp.dot(matrix.astype(jnp.float32), rounded, precision=precise)

    norm_now = jnp.sum(residual * residual, axis=(0, 1))
    for iteration in range(ITERS):
        applied = lax.map(matvec, (schur_blocks, direction))
        curvature = jnp.sum(direction * applied, axis=(0, 1))
        step_size = norm_now / curvature
        residual = residual - step_size * applied
        corner_vals = residual[:, :COR, :].reshape(-1, columns_count)
        coarse = jax.ops.segment_sum(corner_vals, coarse_index, num_segments=PANELS * CB)
        coarse = coarse.reshape(PANELS, CB, columns_count)
        solved = coarse_solve(coarse, panel_order, coarse_factor, block_inverses)
        correction = solved.reshape(PANELS * CB, columns_count)[coarse_index].reshape(sub_count, COR, columns_count)
        corrected = jnp.concatenate([residual[:, :COR, :] + correction, residual[:, COR:, :]], axis=1)
        norm_next = jnp.sum(residual * residual, axis=(0, 1))
        direction = corrected + (norm_next / norm_now) * direction
        norm_now = norm_next
    return residual, direction
```

```python
import functools

import jax
import jax.numpy as jnp
from jax import lax
from jax.experimental import pallas as pl
from jax.experimental.pallas import tpu as pltpu
from jax.sharding import PartitionSpec as P


LANES = 128
exact = lax.Precision.HIGHEST
fine = lax.Precision.HIGH


def swap(value, mask, size):
    return lax.ppermute(value, "blk", [(i, i ^ mask) for i in range(size)])


def across(value):
    return lax.ppermute(value, "grp", [(0, 1), (1, 0)])


def total_over(value, masks, size):
    total = value
    for part in [swap(value, mask, size) for mask in masks]:
        total = total + part
    return total


def times_transposed(left, right, precision):
    return lax.dot_general(
        left,
        right,
        (((1,), (1,)), ((), ())),
        precision=precision,
        preferred_element_type=jnp.float32,
    )


def columns_of_i(ref, lead, place):
    half = ref.shape[-1] // 2
    parts = []
    for top in range(2):
        start = pl.multiple_of(top * half + place * LANES, LANES)
        parts.append(ref[lead + (slice(None), pl.ds(start, LANES))])
    return parts


def columns_of_j(ref, lead, place):
    half = ref.shape[-1] // 2
    top, low = place // 2, place % 2
    rows = ref.shape[-2]
    lane = lax.broadcasted_iota(jnp.int32, (rows, LANES), 1)
    first = lane < LANES // 2
    parts = []
    for pair in range(half // (2 * LANES)):
        picked = []
        for member in range(2):
            start = pl.multiple_of(top * half + (2 * pair + member) * LANES, LANES)
            picked.append(ref[lead + (slice(None), pl.ds(start, LANES))])
        even = jnp.where(first, picked[0], pltpu.roll(picked[1], LANES // 2, 1))
        odd = jnp.where(first, pltpu.roll(picked[0], LANES // 2, 1), picked[1])
        parts.append(jnp.where(low == 0, even, odd))
    return parts


def pack(array, picks, place, core, columns):
    count = picks[0].shape[0]
    rows, width = array.shape[-2:]
    lead = len(picks)
    quarter = width // 4
    scalars = jnp.stack([place, core]).astype(jnp.int32)

    def body(info, *rest):
        first, second, own, *sends = rest[lead:]
        zeros = (0,) * lead
        my_place, my_core = info[0], info[1]
        for slot, source in enumerate((first, second)):
            for at, part in enumerate(columns(source, zeros, my_place)):
                own[slot, :, at * LANES : (at + 1) * LANES] = part
        for code, send in enumerate(sends, start=1):
            for slot, source in enumerate((first, second)):

                @pl.when(my_core == slot)
                def _(code=code, send=send, source=source):
                    for at, part in enumerate(columns(source, zeros, my_place ^ code)):
                        send[0, :, at * LANES : (at + 1) * LANES] = part

    def source_map(slot, step, info, *chosen):
        return tuple(pick[2 * step + slot] for pick in chosen) + (0, 0)

    block = (1,) * lead + (rows, width)
    return pl.pallas_call(
        body,
        out_shape=[jax.ShapeDtypeStruct((count, rows, quarter), jnp.float32)]
        + [jax.ShapeDtypeStruct((count // 2, rows, quarter), jnp.float32)] * 3,
        grid_spec=pltpu.PrefetchScalarGridSpec(
            num_scalar_prefetch=1 + lead,
            grid=(count // 2,),
            in_specs=[pl.BlockSpec(block, functools.partial(source_map, slot)) for slot in range(2)],
            out_specs=[pl.BlockSpec((2, rows, quarter), lambda step, *_: (step, 0, 0))]
            + [pl.BlockSpec((1, rows, quarter), lambda step, *_: (step, 0, 0))] * 3,
        ),
        cost_estimate=pl.CostEstimate(
            flops=0, bytes_accessed=count * rows * width * 6, transcendentals=0
        ),
        name="pack",
    )(scalars, *picks, array, array)


def unpack(own, received, from_core, place, core):
    count, rows, quarter = own.shape
    scalars = jnp.stack([place, core]).astype(jnp.int32)

    def body(info, own_ref, *rest):
        mine, theirs, out = rest[:3], rest[3:6], rest[6]
        my_place, my_core = info[0], info[1]
        for slot in range(2):
            out[slot, pl.ds(pl.multiple_of(my_place * rows, rows), rows), :] = own_ref[slot]
            for code in range(1, 4):
                value = jnp.where(my_core == slot, mine[code - 1][0], theirs[code - 1][0])
                out[slot, pl.ds(pl.multiple_of((my_place ^ code) * rows, rows), rows), :] = value

    single = pl.BlockSpec((1, rows, quarter), lambda step, *_: (step, 0, 0))
    return pl.pallas_call(
        body,
        out_shape=jax.ShapeDtypeStruct((count, 4 * rows, quarter), jnp.float32),
        grid_spec=pltpu.PrefetchScalarGridSpec(
            num_scalar_prefetch=1,
            grid=(count // 2,),
            in_specs=[pl.BlockSpec((2, rows, quarter), lambda step, *_: (step, 0, 0))] + [single] * 6,
            out_specs=pl.BlockSpec((2, 4 * rows, quarter), lambda step, *_: (step, 0, 0)),
        ),
        cost_estimate=pl.CostEstimate(
            flops=0, bytes_accessed=count * rows * quarter * 32, transcendentals=0
        ),
        name="unpack",
    )(scalars, own, *received, *from_core)


def spread(array, picks, place, core, columns, masks, size):
    own, *sends = pack(array, picks, place, core, columns)
    received = [swap(send, mask, size) for send, mask in zip(sends, masks)]
    from_core = [across(value) for value in received]
    return unpack(own, received, from_core, place, core)


def grid_local(size, schur_blocks, residual, direction, corner_map, panel_order, coarse_factor, block_inverses):
    panels, rows_b, width = block_inverses.shape
    sub_count, corners = corner_map.shape
    vectors = residual.shape[-1]
    half = vectors // 2
    quarter = width // 4
    here = sub_count * corners
    device = lax.axis_index("blk")
    core = lax.axis_index("grp")
    place_i = (device // 2) % 4
    place_j = (device // 8) * 2 + device % 2
    masks_i, masks_j = (2, 4, 6), (1, 8, 9)

    inverses = spread(block_inverses, (panel_order,), place_j, core, columns_of_j, masks_j, size)
    coupling = {}
    for low, high in ((1, 4), (4, panels)):
        pairs = [(t, u) for t in range(low, high) for u in range(t)]
        picks = (
            panel_order[jnp.array([t for t, _ in pairs], jnp.int32)],
            panel_order[jnp.array([u for _, u in pairs], jnp.int32)],
        )
        blocks = spread(coarse_factor, picks, place_i, core, columns_of_i, masks_i, size)
        for at, pair in enumerate(pairs):
            coupling[pair] = blocks[at]

    applied = jnp.einsum(
        "sij,sjv->siv", schur_blocks, direction.astype(jnp.bfloat16), preferred_element_type=jnp.float32
    )
    sums = jnp.stack(
        [
            jnp.sum(residual * residual, axis=(0, 1)),
            jnp.sum(direction * applied, axis=(0, 1)),
            jnp.sum(residual * applied, axis=(0, 1)),
            jnp.sum(applied * applied, axis=(0, 1)),
        ]
    )
    corner_res = residual[:, :corners, :].reshape(here, vectors)
    corner_app = applied[:, :corners, :].reshape(here, vectors)
    low_half = jnp.concatenate([corner_res[:, :half], corner_app[:, :half]], axis=1)
    high_half = jnp.concatenate([corner_res[:, half:], corner_app[:, half:]], axis=1)
    slots = corner_map.reshape(1, here).astype(jnp.float32)
    common = jnp.concatenate([sums, jnp.pad(slots, ((0, 3), (0, vectors - here)))], axis=0)
    keep = jnp.where(core == 0, low_half, high_half)
    give = jnp.where(core == 0, high_half, low_half)
    other = across(jnp.concatenate([give, common], axis=0))
    values = jnp.concatenate([keep, other[:here]], axis=0)
    sums = sums + other[here : here + 4]
    slots = jnp.concatenate([slots, other[here + 4 : here + 5, :here]], axis=1).astype(jnp.int32)[0]

    panel, row = slots // rows_b, slots % rows_b
    turn = jnp.sum(
        jnp.where(panel[:, None] == panel_order[None, :], jnp.arange(panels, dtype=jnp.int32)[None, :], 0), axis=1
    )
    columns = lax.broadcasted_iota(jnp.int32, (2 * here, panels * quarter), 1)
    into = (columns == (turn * quarter + place_i * rows_b + row)[:, None]).astype(jnp.float32)
    outof = (columns == (turn * quarter + place_j * rows_b + row)[:, None]).astype(jnp.float32)
    coarse = lax.dot_general(
        values, into, (((0,), (0,)), ((), ())), precision=exact, preferred_element_type=jnp.float32
    )

    with_sums = jnp.concatenate([coarse[:, :quarter], jnp.pad(sums, ((0, 4), (0, quarter - vectors)))], axis=0)
    with_sums = total_over(with_sums, masks_i, size)
    partial = times_transposed(with_sums[:vectors], inverses[0], fine)
    with_sums = jnp.concatenate([partial, with_sums[vectors:]], axis=0)
    with_sums = total_over(with_sums, masks_j, size)
    norm_now, curvature, crossed, squared = (with_sums[vectors + k, :vectors] for k in range(4))
    step_size = norm_now / curvature
    norm_next = norm_now - step_size * (2.0 * crossed - step_size * squared)
    step_half = jnp.where(core == 0, step_size[:half], step_size[half:])[:, None]
    solved = [with_sums[:half] - step_half * with_sums[half:vectors]]
    coarse = coarse[:half] - step_half * coarse[half:]

    pending = [coarse[:, t * quarter : (t + 1) * quarter] for t in range(panels)]
    for t in range(1, panels):
        for later in range(t, panels):
            pending[later] = pending[later] - times_transposed(solved[t - 1], coupling[later, t - 1], fine)
        target = total_over(pending[t], masks_i, size)
        solved.append(total_over(times_transposed(target, inverses[t], fine), masks_j, size))

    correction = 0.0
    for t in range(panels):
        correction = correction + times_transposed(outof[:, t * quarter : (t + 1) * quarter], solved[t], exact)
    other = across(correction[here:])
    correction = jnp.where(
        core == 0,
        jnp.concatenate([correction[:here], other], axis=1),
        jnp.concatenate([other, correction[:here]], axis=1),
    ).reshape(sub_count, corners, vectors)
    residual = residual - step_size * applied
    direction = residual + norm_next / norm_now * direction
    direction = direction.at[:, :corners, :].add(correction)
    return (residual, direction)


def squares(residual):
    return lax.psum(jnp.sum(residual * residual, axis=(0, 1)), ("blk", "grp"))


def solve(coarse, panel_order, coarse_factor, block_inverses):
    panels = coarse.shape[0]
    pending = jnp.zeros_like(coarse)
    solved = jnp.zeros_like(coarse)
    for position in range(panels):
        current = panel_order[position]
        target = lax.dynamic_index_in_dim(coarse - pending, current, 0, keepdims=False)
        inverse = lax.dynamic_index_in_dim(block_inverses, current, 0, keepdims=False)
        block_value = jnp.dot(
            inverse,
            lax.all_gather(target, "blk", axis=0, tiled=True),
            precision=exact,
            preferred_element_type=jnp.float32,
        )
        solved = lax.dynamic_update_index_in_dim(solved, block_value, current, 0)
        if position + 1 < panels:
            coupling = lax.dynamic_index_in_dim(coarse_factor, current, 1, keepdims=False)
            pending = pending + jnp.einsum(
                "aic,cv->aiv", coupling, lax.all_gather(block_value, "blk", axis=0, tiled=True), precision=exact
            )
    return solved


def row_local(schur_blocks, residual, direction, corner_map, panel_order, coarse_factor, block_inverses):
    panels, rows_b = block_inverses.shape[:2]
    sub_count, corners = corner_map.shape
    columns_iota = lax.broadcasted_iota(jnp.int32, (sub_count, corners, panels * rows_b), 2)
    placing = (corner_map[:, :, None] == columns_iota).astype(jnp.float32)
    norm_now = squares(residual)
    applied = jnp.einsum(
        "sij,sjv->siv", schur_blocks, direction.astype(jnp.bfloat16), preferred_element_type=jnp.float32
    )
    curvature = lax.psum(jnp.sum(direction * applied, axis=(0, 1)), ("blk", "grp"))
    residual = residual - norm_now / curvature * applied
    norm_next = squares(residual)
    corner_part = jnp.einsum("scm,scv->mv", placing, residual[:, :corners, :], precision=exact)
    coarse_part = lax.psum(corner_part.reshape(panels, rows_b, -1), "grp")
    solved = solve(coarse_part, panel_order, coarse_factor, block_inverses)
    correction = jnp.einsum("scm,mv->scv", placing, solved.reshape(panels * rows_b, -1), precision=exact)
    direction = (residual + norm_next / norm_now * direction).at[:, :corners, :].add(correction)
    return (residual, direction)


def solution(mesh):
    in_specs = (
        P(("blk", "grp"), None, None),
        P(("blk", "grp"), None, None),
        P(("blk", "grp"), None, None),
        P(("blk", "grp"), None),
        P(),
        P(None, None, "blk", None),
        P(None, "blk", None),
    )
    out_specs = (P(("blk", "grp"), None, None), P(("blk", "grp"), None, None))
    size = mesh.shape["blk"]

    def local(*args):
        rows_b, width = args[-1].shape[1:]
        panels, corners = args[-1].shape[0], args[3].shape[0] * args[3].shape[1]
        as_grid = (
            size == 16
            and mesh.shape["grp"] == 2
            and 2 * rows_b == LANES
            and panels % 2 == 0
            and args[1].shape[-1] == LANES
            and corners % 8 == 0
            and corners <= LANES
        )
        return functools.partial(grid_local, size)(*args) if as_grid else row_local(*args)

    return jax.shard_map(local, mesh=mesh, in_specs=in_specs, out_specs=out_specs, check_vma=False)
```

```python
import jax
import jax.numpy as jnp
from jax import lax
from jax.experimental import pallas as pl
from jax.experimental.pallas import tpu as pltpu
from jax.sharding import PartitionSpec as P


LANES = 128
KERNEL_VMEM = 3 << 20
BATCHES = (
    ("inv_a", 0, 2, None, None, 0),
    ("inv_b", 2, 4, None, 1, 3),
    ("inv_c", 4, 8, None, 5, 8),
    ("low_a", 0, 4, 0, 0, 1),
    ("low_b", 4, 12, 1, 2, 5),
    ("low_c", 12, 20, 1, 4, 7),
    ("low_d", 20, 28, 3, 6, 9),
)
exact = lax.Precision.HIGHEST
fine = lax.Precision.HIGH


def swap(value, mask, size):
    return lax.ppermute(value, "blk", [(i, i ^ mask) for i in range(size)])


def across(value):
    return lax.ppermute(value, "grp", [(0, 1), (1, 0)])


def after(value, other):
    return lax.optimization_barrier((value, other))[0]


def parts_over(values, masks, size):
    return [swap(value, mask, size) for value, mask in zip(values, masks)]


def total_over(value, masks, size):
    parts = parts_over([value] * len(masks), masks, size)
    total = value
    for part in parts:
        total = total + part
    return total


def times_transposed(left, right, precision):
    return lax.dot_general(
        left,
        right,
        (((1,), (1,)), ((), ())),
        precision=precision,
        preferred_element_type=jnp.float32,
    )


def put_columns_of_i(target, ref, slot, place):
    quarter = ref.shape[-1] // 4
    first = lax.broadcasted_iota(jnp.int32, (ref.shape[-2], LANES), 1) < LANES // 2
    for low in range(2):

        @pl.when(place % 2 == low)
        def _(low=low):
            for pair in range(2):
                even, odd = (
                    ref[slot, :, pl.ds(pl.multiple_of(member * quarter + place // 2 * LANES, LANES), LANES)]
                    for member in (2 * pair, 2 * pair + 1)
                )
                even, odd = (pltpu.roll(even, LANES // 2, 1), odd) if low else (even, pltpu.roll(odd, LANES // 2, 1))
                target[:, pair * LANES : (pair + 1) * LANES] = jnp.where(first, even, odd)


def put_columns_of_j(target, ref, slot, place):
    quarter = ref.shape[-1] // 4
    target[...] = ref[slot, :, pl.ds(pl.multiple_of(place * quarter, quarter), quarter)]


def pack(array, order, groups, place, core, columns, earlier):
    rows, width = array.shape[-2:]
    quarter = width // 4
    total = sum(len(group) for group in groups)
    scalars = jnp.stack([place, core]).astype(jnp.int32)
    if earlier is not None:
        scalars = after(scalars, earlier)

    def body(info, turns, source, *rest):
        outs, held, arrived = rest[:-2], rest[-2], rest[-1]
        my_place, my_core = info[0], info[1]
        copies = []
        for picks in [picks for group in groups for picks in group]:
            block = source
            for pick in picks:
                block = block.at[turns[pick]]
            slot = len(copies)
            copies.append(pltpu.make_async_copy(block, held.at[slot], arrived.at[slot]))
            copies[-1].start()

        def put(target, at, slot, whose):
            columns(target.at[at], held, slot, whose)

        slot = 0
        for number, group in enumerate(groups):
            own, near, far = outs[3 * number : 3 * number + 3]
            for at in range(len(group)):
                copies[slot].wait()
                put(own, at, slot, my_place)
                put(near, at, slot, my_place ^ (1 + my_core))

                @pl.when(my_core == at % 2)
                def _(far=far, at=at, slot=slot):
                    put(far, at // 2, slot, my_place ^ 3)

                slot += 1

    shapes = [(count, rows, quarter) for group in groups for count in (len(group), len(group), len(group) // 2)]
    outs = pl.pallas_call(
        body,
        out_shape=[jax.ShapeDtypeStruct(shape, jnp.float32) for shape in shapes],
        grid_spec=pltpu.PrefetchScalarGridSpec(
            num_scalar_prefetch=2,
            grid=(1,),
            in_specs=[pl.BlockSpec(memory_space=pltpu.HBM)],
            out_specs=[pl.BlockSpec(shape, lambda *_: (0, 0, 0)) for shape in shapes],
            scratch_shapes=[pltpu.VMEM((total, rows, width), jnp.float32), pltpu.SemaphoreType.DMA((total,))],
        ),
        cost_estimate=pl.CostEstimate(flops=0, bytes_accessed=total * rows * width * 6, transcendentals=0),
        compiler_params=pltpu.CompilerParams(vmem_limit_bytes=KERNEL_VMEM + total * rows * width * 10),
        name="pack",
    )(scalars, order, pltpu.with_memory_space_constraint(array, pltpu.HBM))
    return [outs[3 * number : 3 * number + 3] for number in range(len(groups))]


def unpack(own, near, far, place, core):
    count, rows, quarter = own.shape
    scalars = jnp.stack([place, core]).astype(jnp.int32)

    def body(info, own_ref, near_ref, near_other, far_ref, far_other, out):
        my_place, my_core = info[0], info[1]

        def put(slot, code, value):
            out[slot, pl.ds(pl.multiple_of((my_place ^ code) * rows, rows), rows), :] = value

        for slot in range(2):
            put(slot, 0, own_ref[slot])
            put(slot, 1 + my_core, near_ref[slot])
            put(slot, 2 - my_core, near_other[slot])
            put(slot, 3, jnp.where(my_core == slot, far_ref[0], far_other[0]))

    single = pl.BlockSpec((1, rows, quarter), lambda step, *_: (step, 0, 0))
    double = pl.BlockSpec((2, rows, quarter), lambda step, *_: (step, 0, 0))
    return pl.pallas_call(
        body,
        out_shape=jax.ShapeDtypeStruct((count, 4 * rows, quarter), jnp.float32),
        grid_spec=pltpu.PrefetchScalarGridSpec(
            num_scalar_prefetch=1,
            grid=(count // 2,),
            in_specs=[double, double, double, single, single],
            out_specs=pl.BlockSpec((2, 4 * rows, quarter), lambda step, *_: (step, 0, 0)),
        ),
        cost_estimate=pl.CostEstimate(flops=0, bytes_accessed=count * rows * quarter * 32, transcendentals=0),
        compiler_params=pltpu.CompilerParams(vmem_limit_bytes=KERNEL_VMEM),
        name="unpack",
    )(scalars, own, *near, *far)


def exchange(packed, masks, size, place, core):
    own, near, far = packed
    routes = [(2 * i + c, 2 * (i ^ masks[c]) + c) for i in range(size) for c in range(2)]
    near = lax.ppermute(near, ("blk", "grp"), routes)
    far = swap(far, masks[2], size)
    near_other, far_other = across(near), across(far)
    return unpack(own, (near, near_other), (far, far_other), place, core)


def grid_local(size, schur_blocks, residual, direction, corner_map, panel_order, coarse_factor, block_inverses):
    panels, rows_b, width = block_inverses.shape
    sub_count, corners = corner_map.shape
    vectors = residual.shape[-1]
    half = vectors // 2
    quarter = width // 4
    here = sub_count * corners
    device = lax.axis_index("blk")
    core = lax.axis_index("grp")
    place_i, place_j = device % 4, device // 4
    masks_i, masks_j = (1, 2, 3), (4, 8, 12)

    inverses, coupling, packed = {}, {}, {}
    pairs = [(t, u) for t in range(panels) for u in range(t)]

    def at_step(step, message):
        for kind in ("inv", "low"):
            chosen = [batch for batch in BATCHES if batch[0].startswith(kind) and batch[3] == step]
            if not chosen:
                continue
            if kind == "inv":
                groups = [[(t,) for t in range(low, high)] for _, low, high, *_ in chosen]
                how = (block_inverses, panel_order, groups, place_j, core, put_columns_of_j, message)
            else:
                groups = [pairs[low:high] for _, low, high, *_ in chosen]
                how = (coarse_factor, panel_order, groups, place_i, core, put_columns_of_i, message)
            packed.update(zip([batch[0] for batch in chosen], pack(*how)))
        for name, low, high, packing, sending, _ in BATCHES:
            if sending != step:
                continue
            ready = packed[name]
            if packing != sending:
                ready = [*ready[:1], *after(tuple(ready[1:]), message)]
            if name.startswith("inv"):
                blocks = exchange(ready, masks_j, size, place_j, core)
                inverses.update({low + at: blocks[at] for at in range(high - low)})
            else:
                blocks = exchange(ready, masks_i, size, place_i, core)
                coupling.update({pair: blocks[at] for at, pair in enumerate(pairs[low:high])})

    at_step(None, None)

    applied = jnp.einsum(
        "sij,sjv->siv", schur_blocks, direction.astype(jnp.bfloat16), preferred_element_type=jnp.float32
    )
    sums = jnp.stack(
        [
            jnp.sum(residual * residual, axis=(0, 1)),
            jnp.sum(direction * applied, axis=(0, 1)),
            jnp.sum(residual * applied, axis=(0, 1)),
            jnp.sum(applied * applied, axis=(0, 1)),
        ]
    )
    corner_res = residual[:, :corners, :].reshape(here, vectors)
    corner_app = applied[:, :corners, :].reshape(here, vectors)
    low_half = jnp.concatenate([corner_res[:, :half], corner_app[:, :half]], axis=1)
    high_half = jnp.concatenate([corner_res[:, half:], corner_app[:, half:]], axis=1)
    slots = corner_map.reshape(1, here).astype(jnp.float32)
    common = jnp.concatenate([sums, jnp.pad(slots, ((0, 3), (0, vectors - here)))], axis=0)
    keep = jnp.where(core == 0, low_half, high_half)
    give = jnp.where(core == 0, high_half, low_half)
    other = across(jnp.concatenate([give, common], axis=0))
    values = jnp.concatenate([keep, other[:here]], axis=0)
    sums = sums + other[here : here + 4]
    slots = jnp.concatenate([slots, other[here + 4 : here + 5, :here]], axis=1).astype(jnp.int32)[0]

    panel, row = slots // rows_b, slots % rows_b
    turn = jnp.sum(
        jnp.where(panel[:, None] == panel_order[None, :], jnp.arange(panels, dtype=jnp.int32)[None, :], 0), axis=1
    )
    columns = lax.broadcasted_iota(jnp.int32, (2 * here, panels * quarter), 1)
    into = (columns == (turn * quarter + place_i * rows_b + row)[:, None]).astype(jnp.float32)
    outof = (columns == (turn * quarter + place_j * rows_b + row)[:, None]).astype(jnp.float32)
    coarse = lax.dot_general(
        values, into, (((0,), (0,)), ((), ())), precision=exact, preferred_element_type=jnp.float32
    )

    pairwise = lax.broadcasted_iota(jnp.int32, (2 * here, 2 * rows_b), 1)
    into_first = (turn == 0)[:, None] & (pairwise == (place_i % 2 * rows_b + row)[:, None])
    first = lax.dot_general(
        values,
        into_first.astype(jnp.float32),
        (((0,), (0,)), ((), ())),
        precision=exact,
        preferred_element_type=jnp.float32,
    )
    first = jnp.concatenate([first, jnp.pad(sums, ((0, 4), (0, 0)))], axis=0)
    at_step(0, first)
    parts = parts_over([first] * 3, masks_i, size)
    same, other = first + parts[0], parts[1] + parts[2]
    in_low = place_i // 2 == 0
    with_sums = jnp.concatenate([jnp.where(in_low, same, other), jnp.where(in_low, other, same)], axis=1)
    sums = same[vectors:] + other[vectors:]
    partial = times_transposed(with_sums[:vectors], inverses[0], fine)
    with_sums = jnp.concatenate([partial, jnp.pad(sums, ((0, 0), (0, quarter - vectors)))], axis=0)
    at_step(1, with_sums)
    at_step("1b", with_sums)
    with_sums = total_over(with_sums, masks_j, size)
    norm_now, curvature, crossed, squared = (with_sums[vectors + k, :vectors] for k in range(4))
    step_size = norm_now / curvature
    norm_next = norm_now - step_size * (2.0 * crossed - step_size * squared)
    residual = residual - step_size * applied
    residual, moved = lax.optimization_barrier((residual, residual + norm_next / norm_now * direction))
    step_half = jnp.where(core == 0, step_size[:half], step_size[half:])[:, None]
    solved = [with_sums[:half] - step_half * with_sums[half:vectors]]
    coarse = coarse[:half] - step_half * coarse[half:]

    for t in range(1, panels):
        target = coarse[:, t * quarter : (t + 1) * quarter]
        for u in range(t - 1):
            target = target - times_transposed(solved[u], coupling[t, u], fine)
        target = lax.optimization_barrier(target)
        target = target - times_transposed(solved[t - 1], coupling[t, t - 1], fine)
        at_step(2 * t, target)
        target = total_over(target, masks_i, size)
        partial = times_transposed(target, inverses[t], fine)
        at_step(2 * t + 1, partial)
        if t + 1 < panels:
            solved.append(total_over(partial, masks_j, size))

    halves = partial[:, : 2 * rows_b], partial[:, 2 * rows_b :]
    own_low = place_j // 2 == 0
    mine, others = jnp.where(own_low, halves[0], halves[1]), jnp.where(own_low, halves[1], halves[0])
    parts = parts_over([mine, others, others], masks_j, size)
    last = mine + parts[0] + parts[1] + parts[2]
    outof_last = (turn == panels - 1)[:, None] & (pairwise == (place_j % 2 * rows_b + row)[:, None])

    correction = 0.0
    for t in range(panels - 1):
        correction = correction + times_transposed(outof[:, t * quarter : (t + 1) * quarter], solved[t], exact)
    correction = lax.optimization_barrier(correction)
    correction = correction + times_transposed(outof_last.astype(jnp.float32), last, exact)
    other = across(correction[here:])
    correction = jnp.where(
        core == 0,
        jnp.concatenate([correction[:here], other], axis=1),
        jnp.concatenate([other, correction[:here]], axis=1),
    ).reshape(sub_count, corners, vectors)
    return (residual, moved.at[:, :corners, :].add(correction))


def squares(residual):
    return lax.psum(jnp.sum(residual * residual, axis=(0, 1)), ("blk", "grp"))


def solve(coarse, panel_order, coarse_factor, block_inverses):
    panels = coarse.shape[0]
    pending = jnp.zeros_like(coarse)
    solved = jnp.zeros_like(coarse)
    for position in range(panels):
        current = panel_order[position]
        target = lax.dynamic_index_in_dim(coarse - pending, current, 0, keepdims=False)
        inverse = lax.dynamic_index_in_dim(block_inverses, current, 0, keepdims=False)
        block_value = jnp.dot(
            inverse,
            lax.all_gather(target, "blk", axis=0, tiled=True),
            precision=exact,
            preferred_element_type=jnp.float32,
        )
        solved = lax.dynamic_update_index_in_dim(solved, block_value, current, 0)
        if position + 1 < panels:
            coupling = lax.dynamic_index_in_dim(coarse_factor, current, 1, keepdims=False)
            pending = pending + jnp.einsum(
                "aic,cv->aiv", coupling, lax.all_gather(block_value, "blk", axis=0, tiled=True), precision=exact
            )
    return solved


def row_local(schur_blocks, residual, direction, corner_map, panel_order, coarse_factor, block_inverses):
    panels, rows_b = block_inverses.shape[:2]
    sub_count, corners = corner_map.shape
    columns_iota = lax.broadcasted_iota(jnp.int32, (sub_count, corners, panels * rows_b), 2)
    placing = (corner_map[:, :, None] == columns_iota).astype(jnp.float32)
    norm_now = squares(residual)
    applied = jnp.einsum(
        "sij,sjv->siv", schur_blocks, direction.astype(jnp.bfloat16), preferred_element_type=jnp.float32
    )
    curvature = lax.psum(jnp.sum(direction * applied, axis=(0, 1)), ("blk", "grp"))
    residual = residual - norm_now / curvature * applied
    norm_next = squares(residual)
    corner_part = jnp.einsum("scm,scv->mv", placing, residual[:, :corners, :], precision=exact)
    coarse_part = lax.psum(corner_part.reshape(panels, rows_b, -1), "grp")
    solved = solve(coarse_part, panel_order, coarse_factor, block_inverses)
    correction = jnp.einsum("scm,mv->scv", placing, solved.reshape(panels * rows_b, -1), precision=exact)
    direction = (residual + norm_next / norm_now * direction).at[:, :corners, :].add(correction)
    return (residual, direction)


def solution(mesh):
    in_specs = (
        P(("blk", "grp"), None, None),
        P(("blk", "grp"), None, None),
        P(("blk", "grp"), None, None),
        P(("blk", "grp"), None),
        P(),
        P(None, None, "blk", None),
        P(None, "blk", None),
    )
    out_specs = (P(("blk", "grp"), None, None), P(("blk", "grp"), None, None))
    size = mesh.shape["blk"]

    def local(*args):
        rows_b, _ = args[-1].shape[1:]
        panels, corners = args[-1].shape[0], args[3].shape[0] * args[3].shape[1]
        as_grid = (
            size == 16
            and mesh.shape["grp"] == 2
            and 2 * rows_b == LANES
            and panels % 2 == 0
            and args[1].shape[-1] == LANES
            and corners % 8 == 0
            and corners <= LANES
        )
        return grid_local(size, *args) if as_grid else row_local(*args)

    return jax.shard_map(local, mesh=mesh, in_specs=in_specs, out_specs=out_specs, check_vma=False)
```

```python
import jax
import jax.numpy as jnp
from jax import lax
from jax.experimental import pallas as pl
from jax.experimental.pallas import tpu as pltpu
from jax.sharding import PartitionSpec as P


LANES = 128
KERNEL_VMEM = 3 << 20
BATCHES = (
    ("inv_a", 0, 2, None, None, 0),
    ("inv_b", 2, 4, None, 1, 3),
    ("inv_c", 4, 8, None, 5, 8),
    ("low_a", 0, 4, 0, 0, 1),
    ("low_b", 4, 12, 1, 2, 5),
    ("low_c", 12, 20, 1, 4, 7),
    ("low_d", 20, 28, 3, 6, 9),
)
exact = lax.Precision.HIGHEST
fine = lax.Precision.HIGH


def swap(value, mask, size):
    return lax.ppermute(value, "blk", [(i, i ^ mask) for i in range(size)])


def across(value):
    return lax.ppermute(value, "grp", [(0, 1), (1, 0)])


def after(value, other):
    return lax.optimization_barrier((value, other))[0]


def parts_over(values, masks, size):
    return [swap(value, mask, size) for value, mask in zip(values, masks)]


def total_over(value, masks, size):
    parts = parts_over([value] * len(masks), masks, size)
    total = value
    for part in parts:
        total = total + part
    return total


def times_transposed(left, right, precision):
    return lax.dot_general(
        left,
        right,
        (((1,), (1,)), ((), ())),
        precision=precision,
        preferred_element_type=jnp.float32,
    )


def put_columns_of_i(target, ref, slot, place):
    quarter = ref.shape[-1] // 4
    first = lax.broadcasted_iota(jnp.int32, (ref.shape[-2], LANES), 1) < LANES // 2
    for low in range(2):

        @pl.when(place % 2 == low)
        def _(low=low):
            for pair in range(2):
                even, odd = (
                    ref[slot, :, pl.ds(pl.multiple_of(member * quarter + place // 2 * LANES, LANES), LANES)]
                    for member in (2 * pair, 2 * pair + 1)
                )
                even, odd = (pltpu.roll(even, LANES // 2, 1), odd) if low else (even, pltpu.roll(odd, LANES // 2, 1))
                target[:, pair * LANES : (pair + 1) * LANES] = jnp.where(first, even, odd)


def put_columns_of_j(target, ref, slot, place):
    quarter = ref.shape[-1] // 4
    target[...] = ref[slot, :, pl.ds(pl.multiple_of(place * quarter, quarter), quarter)]


def pack(array, order, groups, place, core, columns, earlier):
    rows, width = array.shape[-2:]
    quarter = width // 4
    total = sum(len(group) for group in groups)
    scalars = jnp.stack([place, core]).astype(jnp.int32)
    if earlier is not None:
        scalars = after(scalars, earlier)

    def body(info, turns, source, *rest):
        outs, held, arrived = rest[:-2], rest[-2], rest[-1]
        my_place, my_core = info[0], info[1]
        copies = []
        for picks in [picks for group in groups for picks in group]:
            block = source
            for pick in picks:
                block = block.at[turns[pick]]
            slot = len(copies)
            copies.append(pltpu.make_async_copy(block, held.at[slot], arrived.at[slot]))
            copies[-1].start()

        def put(target, at, slot, whose):
            columns(target.at[at], held, slot, whose)

        slot = 0
        for number, group in enumerate(groups):
            own, near, far = outs[3 * number : 3 * number + 3]
            for at in range(len(group)):
                copies[slot].wait()
                put(own, at, slot, my_place)
                put(near, at, slot, my_place ^ (1 + my_core))

                @pl.when(my_core == at % 2)
                def _(far=far, at=at, slot=slot):
                    put(far, at // 2, slot, my_place ^ 3)

                slot += 1

    shapes = [(count, rows, quarter) for group in groups for count in (len(group), len(group), len(group) // 2)]
    outs = pl.pallas_call(
        body,
        out_shape=[jax.ShapeDtypeStruct(shape, jnp.float32) for shape in shapes],
        grid_spec=pltpu.PrefetchScalarGridSpec(
            num_scalar_prefetch=2,
            grid=(1,),
            in_specs=[pl.BlockSpec(memory_space=pltpu.HBM)],
            out_specs=[pl.BlockSpec(shape, lambda *_: (0, 0, 0)) for shape in shapes],
            scratch_shapes=[pltpu.VMEM((total, rows, width), jnp.float32), pltpu.SemaphoreType.DMA((total,))],
        ),
        cost_estimate=pl.CostEstimate(flops=0, bytes_accessed=total * rows * width * 6, transcendentals=0),
        compiler_params=pltpu.CompilerParams(vmem_limit_bytes=KERNEL_VMEM + total * rows * width * 10),
        name="pack",
    )(scalars, order, pltpu.with_memory_space_constraint(array, pltpu.HBM))
    return [outs[3 * number : 3 * number + 3] for number in range(len(groups))]


def unpack(own, near, far, place, core):
    count, rows, quarter = own.shape
    scalars = jnp.stack([place, core]).astype(jnp.int32)

    def body(info, own_ref, near_ref, near_other, far_ref, far_other, out):
        my_place, my_core = info[0], info[1]

        def put(slot, code, value):
            out[slot, pl.ds(pl.multiple_of((my_place ^ code) * rows, rows), rows), :] = value

        for slot in range(2):
            put(slot, 0, own_ref[slot])
            put(slot, 1 + my_core, near_ref[slot])
            put(slot, 2 - my_core, near_other[slot])
            put(slot, 3, jnp.where(my_core == slot, far_ref[0], far_other[0]))

    single = pl.BlockSpec((1, rows, quarter), lambda step, *_: (step, 0, 0))
    double = pl.BlockSpec((2, rows, quarter), lambda step, *_: (step, 0, 0))
    return pl.pallas_call(
        body,
        out_shape=jax.ShapeDtypeStruct((count, 4 * rows, quarter), jnp.float32),
        grid_spec=pltpu.PrefetchScalarGridSpec(
            num_scalar_prefetch=1,
            grid=(count // 2,),
            in_specs=[double, double, double, single, single],
            out_specs=pl.BlockSpec((2, 4 * rows, quarter), lambda step, *_: (step, 0, 0)),
        ),
        cost_estimate=pl.CostEstimate(flops=0, bytes_accessed=count * rows * quarter * 32, transcendentals=0),
        compiler_params=pltpu.CompilerParams(vmem_limit_bytes=KERNEL_VMEM),
        name="unpack",
    )(scalars, own, *near, *far)


def exchange(packed, masks, size, place, core):
    own, near, far = packed
    routes = [(2 * i + c, 2 * (i ^ masks[c]) + c) for i in range(size) for c in range(2)]
    near = lax.ppermute(near, ("blk", "grp"), routes)
    far = swap(far, masks[2], size)
    near_other, far_other = across(near), across(far)
    return unpack(own, (near, near_other), (far, far_other), place, core)


def grid_local(size, schur_blocks, residual, direction, corner_map, panel_order, coarse_factor, block_inverses):
    panels, rows_b, width = block_inverses.shape
    sub_count, corners = corner_map.shape
    vectors = residual.shape[-1]
    half = vectors // 2
    quarter = width // 4
    here = sub_count * corners
    device = lax.axis_index("blk")
    core = lax.axis_index("grp")
    place_i, place_j = device % 4, device // 4
    masks_i, masks_j = (1, 2, 3), (4, 8, 12)

    inverses, coupling, packed = {}, {}, {}
    pairs = [(t, u) for t in range(panels) for u in range(t)]

    def at_step(step, message):
        for kind in ("inv", "low"):
            chosen = [batch for batch in BATCHES if batch[0].startswith(kind) and batch[3] == step]
            if not chosen:
                continue
            if kind == "inv":
                groups = [[(t,) for t in range(low, high)] for _, low, high, *_ in chosen]
                how = (block_inverses, panel_order, groups, place_j, core, put_columns_of_j, message)
            else:
                groups = [pairs[low:high] for _, low, high, *_ in chosen]
                how = (coarse_factor, panel_order, groups, place_i, core, put_columns_of_i, message)
            packed.update(zip([batch[0] for batch in chosen], pack(*how)))
        for name, low, high, packing, sending, _ in BATCHES:
            if sending != step:
                continue
            ready = packed[name]
            if packing != sending:
                ready = [*ready[:1], *after(tuple(ready[1:]), message)]
            if name.startswith("inv"):
                blocks = exchange(ready, masks_j, size, place_j, core)
                inverses.update({low + at: blocks[at] for at in range(high - low)})
            else:
                blocks = exchange(ready, masks_i, size, place_i, core)
                coupling.update({pair: blocks[at] for at, pair in enumerate(pairs[low:high])})

    at_step(None, None)

    applied = jnp.einsum(
        "sij,sjv->siv", schur_blocks, direction.astype(jnp.bfloat16), preferred_element_type=jnp.float32
    )
    sums = jnp.stack(
        [
            jnp.sum(residual * residual, axis=(0, 1)),
            jnp.sum(direction * applied, axis=(0, 1)),
            jnp.sum(residual * applied, axis=(0, 1)),
            jnp.sum(applied * applied, axis=(0, 1)),
        ]
    )
    corner_res = residual[:, :corners, :].reshape(here, vectors)
    corner_app = applied[:, :corners, :].reshape(here, vectors)
    low_half = jnp.concatenate([corner_res[:, :half], corner_app[:, :half]], axis=1)
    high_half = jnp.concatenate([corner_res[:, half:], corner_app[:, half:]], axis=1)
    own_slots = corner_map.reshape(here)
    turn = jnp.sum(
        jnp.where(
            (own_slots // rows_b)[:, None] == panel_order[None, :], jnp.arange(panels, dtype=jnp.int32)[None, :], 0
        ),
        axis=1,
    )
    slots = (turn * rows_b + own_slots % rows_b).reshape(1, here).astype(jnp.float32)
    common = jnp.concatenate([sums, jnp.pad(slots, ((0, 3), (0, vectors - here)))], axis=0)
    keep = jnp.where(core == 0, low_half, high_half)
    give = jnp.where(core == 0, high_half, low_half)
    other = across(jnp.concatenate([give, common], axis=0))
    values = jnp.concatenate([keep, other[:here]], axis=0)
    sums = sums + other[here : here + 4]
    slots = jnp.concatenate([slots, other[here + 4 : here + 5, :here]], axis=1).astype(jnp.int32)[0][:, None]

    columns = lax.broadcasted_iota(jnp.int32, (1, panels * quarter), 1)
    column_slot = columns // quarter * rows_b + columns % rows_b
    column_place = columns % quarter // rows_b
    into = (slots == jnp.where(column_place == place_i, column_slot, -1)).astype(jnp.float32)
    outof = (slots == jnp.where(column_place == place_j, column_slot, -1)).astype(jnp.float32)
    coarse = lax.dot_general(
        values, into, (((0,), (0,)), ((), ())), precision=exact, preferred_element_type=jnp.float32
    )

    pairwise = lax.broadcasted_iota(jnp.int32, (1, 2 * rows_b), 1)
    into_first = slots == jnp.where(pairwise // rows_b == place_i % 2, pairwise % rows_b, -1)
    first = lax.dot_general(
        values,
        into_first.astype(jnp.float32),
        (((0,), (0,)), ((), ())),
        precision=exact,
        preferred_element_type=jnp.float32,
    )
    first = jnp.concatenate([first, jnp.pad(sums, ((0, 4), (0, 0)))], axis=0)
    at_step(0, first)
    parts = parts_over([first] * 3, masks_i, size)
    same, other = first + parts[0], parts[1] + parts[2]
    in_low = place_i // 2 == 0
    with_sums = jnp.concatenate([jnp.where(in_low, same, other), jnp.where(in_low, other, same)], axis=1)
    sums = same[vectors:] + other[vectors:]
    partial = times_transposed(with_sums[:vectors], inverses[0], fine)
    with_sums = jnp.concatenate([partial, jnp.pad(sums, ((0, 0), (0, quarter - vectors)))], axis=0)
    at_step(1, with_sums)
    at_step("1b", with_sums)
    with_sums = total_over(with_sums, masks_j, size)
    norm_now, curvature, crossed, squared = (with_sums[vectors + k, :vectors] for k in range(4))
    step_size = norm_now / curvature
    norm_next = norm_now - step_size * (2.0 * crossed - step_size * squared)
    residual = residual - step_size * applied
    residual, moved = lax.optimization_barrier((residual, residual + norm_next / norm_now * direction))
    step_half = jnp.where(core == 0, step_size[:half], step_size[half:])[:, None]
    solved = [with_sums[:half] - step_half * with_sums[half:vectors]]
    coarse = coarse[:half] - step_half * coarse[half:]

    for t in range(1, panels):
        target = coarse[:, t * quarter : (t + 1) * quarter]
        for u in range(t - 1):
            target = target - times_transposed(solved[u], coupling[t, u], fine)
        target = lax.optimization_barrier(target)
        target = target - times_transposed(solved[t - 1], coupling[t, t - 1], fine)
        at_step(2 * t, target)
        target = total_over(target, masks_i, size)
        partial = times_transposed(target, inverses[t], fine)
        at_step(2 * t + 1, partial)
        if t + 1 < panels:
            solved.append(total_over(partial, masks_j, size))

    halves = partial[:, : 2 * rows_b], partial[:, 2 * rows_b :]
    own_low = place_j // 2 == 0
    mine, others = jnp.where(own_low, halves[0], halves[1]), jnp.where(own_low, halves[1], halves[0])
    parts = parts_over([mine, others, others], masks_j, size)
    last = mine + parts[0] + parts[1] + parts[2]
    last_slot = (panels - 1) * rows_b + pairwise % rows_b
    outof_last = slots == jnp.where(pairwise // rows_b == place_j % 2, last_slot, -1)

    correction = 0.0
    for t in range(panels - 1):
        correction = correction + times_transposed(outof[:, t * quarter : (t + 1) * quarter], solved[t], exact)
    correction = lax.optimization_barrier(correction)
    correction = correction + times_transposed(outof_last.astype(jnp.float32), last, exact)
    other = across(correction[here:])
    correction = jnp.where(
        core == 0,
        jnp.concatenate([correction[:here], other], axis=1),
        jnp.concatenate([other, correction[:here]], axis=1),
    ).reshape(sub_count, corners, vectors)
    return (residual, moved.at[:, :corners, :].add(correction))


def squares(residual):
    return lax.psum(jnp.sum(residual * residual, axis=(0, 1)), ("blk", "grp"))


def solve(coarse, panel_order, coarse_factor, block_inverses):
    panels = coarse.shape[0]
    pending = jnp.zeros_like(coarse)
    solved = jnp.zeros_like(coarse)
    for position in range(panels):
        current = panel_order[position]
        target = lax.dynamic_index_in_dim(coarse - pending, current, 0, keepdims=False)
        inverse = lax.dynamic_index_in_dim(block_inverses, current, 0, keepdims=False)
        block_value = jnp.dot(
            inverse,
            lax.all_gather(target, "blk", axis=0, tiled=True),
            precision=exact,
            preferred_element_type=jnp.float32,
        )
        solved = lax.dynamic_update_index_in_dim(solved, block_value, current, 0)
        if position + 1 < panels:
            coupling = lax.dynamic_index_in_dim(coarse_factor, current, 1, keepdims=False)
            pending = pending + jnp.einsum(
                "aic,cv->aiv", coupling, lax.all_gather(block_value, "blk", axis=0, tiled=True), precision=exact
            )
    return solved


def row_local(schur_blocks, residual, direction, corner_map, panel_order, coarse_factor, block_inverses):
    panels, rows_b = block_inverses.shape[:2]
    sub_count, corners = corner_map.shape
    columns_iota = lax.broadcasted_iota(jnp.int32, (sub_count, corners, panels * rows_b), 2)
    placing = (corner_map[:, :, None] == columns_iota).astype(jnp.float32)
    norm_now = squares(residual)
    applied = jnp.einsum(
        "sij,sjv->siv", schur_blocks, direction.astype(jnp.bfloat16), preferred_element_type=jnp.float32
    )
    curvature = lax.psum(jnp.sum(direction * applied, axis=(0, 1)), ("blk", "grp"))
    residual = residual - norm_now / curvature * applied
    norm_next = squares(residual)
    corner_part = jnp.einsum("scm,scv->mv", placing, residual[:, :corners, :], precision=exact)
    coarse_part = lax.psum(corner_part.reshape(panels, rows_b, -1), "grp")
    solved = solve(coarse_part, panel_order, coarse_factor, block_inverses)
    correction = jnp.einsum("scm,mv->scv", placing, solved.reshape(panels * rows_b, -1), precision=exact)
    direction = (residual + norm_next / norm_now * direction).at[:, :corners, :].add(correction)
    return (residual, direction)


def solution(mesh):
    in_specs = (
        P(("blk", "grp"), None, None),
        P(("blk", "grp"), None, None),
        P(("blk", "grp"), None, None),
        P(("blk", "grp"), None),
        P(),
        P(None, None, "blk", None),
        P(None, "blk", None),
    )
    out_specs = (P(("blk", "grp"), None, None), P(("blk", "grp"), None, None))
    size = mesh.shape["blk"]

    def local(*args):
        rows_b, _ = args[-1].shape[1:]
        panels, corners = args[-1].shape[0], args[3].shape[0] * args[3].shape[1]
        as_grid = (
            size == 16
            and mesh.shape["grp"] == 2
            and 2 * rows_b == LANES
            and panels % 2 == 0
            and args[1].shape[-1] == LANES
            and corners % 8 == 0
            and corners <= LANES
        )
        return grid_local(size, *args) if as_grid else row_local(*args)

    return jax.shard_map(local, mesh=mesh, in_specs=in_specs, out_specs=out_specs, check_vma=False)
```

```python
import jax
import jax.numpy as jnp
from jax import lax
from jax.experimental import pallas as pl
from jax.experimental.pallas import tpu as pltpu
from jax.sharding import PartitionSpec as P


LANES = 128
KERNEL_VMEM = 3 << 20
BATCHES = (
    ("inv_a", 0, 2, None, None, 0),
    ("inv_b", 2, 4, 1, 1, 3),
    ("inv_c", 4, 8, 1, 5, 8),
    ("low_a", 0, 4, 0, 0, 1),
    ("low_b", 4, 12, 1, 2, 5),
    ("low_c", 12, 20, 2, 4, 7),
    ("low_d", 20, 28, 3, 6, 9),
)
exact = lax.Precision.HIGHEST
fine = lax.Precision.HIGH


def swap(value, mask, size):
    return lax.ppermute(value, "blk", [(i, i ^ mask) for i in range(size)])


def across(value):
    return lax.ppermute(value, "grp", [(0, 1), (1, 0)])


def after(value, other):
    return lax.optimization_barrier((value, other))[0]


def parts_over(values, masks, size):
    return [swap(value, mask, size) for value, mask in zip(values, masks)]


def total_over(value, masks, size):
    parts = parts_over([value] * len(masks), masks, size)
    total = value
    for part in parts:
        total = total + part
    return total


def times_transposed(left, right, precision):
    return lax.dot_general(
        left,
        right,
        (((1,), (1,)), ((), ())),
        precision=precision,
        preferred_element_type=jnp.float32,
    )


def put_columns_of_i(target, ref, slot, place):
    quarter = ref.shape[-1] // 4
    first = lax.broadcasted_iota(jnp.int32, (ref.shape[-2], LANES), 1) < LANES // 2
    for low in range(2):

        @pl.when(place % 2 == low)
        def _(low=low):
            for pair in range(2):
                even, odd = (
                    ref[slot, :, pl.ds(pl.multiple_of(member * quarter + place // 2 * LANES, LANES), LANES)]
                    for member in (2 * pair, 2 * pair + 1)
                )
                even, odd = (pltpu.roll(even, LANES // 2, 1), odd) if low else (even, pltpu.roll(odd, LANES // 2, 1))
                target[:, pair * LANES : (pair + 1) * LANES] = jnp.where(first, even, odd)


def put_columns_of_j(target, ref, slot, place):
    quarter = ref.shape[-1] // 4
    target[...] = ref[slot, :, pl.ds(pl.multiple_of(place * quarter, quarter), quarter)]


def pack(array, order, groups, place, core, columns, earlier):
    rows, width = array.shape[-2:]
    quarter = width // 4
    total = sum(len(group) for group in groups)
    scalars = jnp.stack([place, core]).astype(jnp.int32)
    if earlier is not None:
        scalars = after(scalars, earlier)

    def body(info, turns, source, *rest):
        outs, held, arrived = rest[:-2], rest[-2], rest[-1]
        my_place, my_core = info[0], info[1]
        copies = []
        for picks in [picks for group in groups for picks in group]:
            block = source
            for pick in picks:
                block = block.at[turns[pick]]
            slot = len(copies)
            copies.append(pltpu.make_async_copy(block, held.at[slot], arrived.at[slot]))
            copies[-1].start()

        def put(target, at, slot, whose):
            columns(target.at[at], held, slot, whose)

        slot = 0
        for number, group in enumerate(groups):
            own, near, far = outs[3 * number : 3 * number + 3]
            for at in range(len(group)):
                copies[slot].wait()
                put(own, at, slot, my_place)
                put(near, at, slot, my_place ^ (1 + my_core))

                @pl.when(my_core == at % 2)
                def _(far=far, at=at, slot=slot):
                    put(far, at // 2, slot, my_place ^ 3)

                slot += 1

    shapes = [(count, rows, quarter) for group in groups for count in (len(group), len(group), len(group) // 2)]
    outs = pl.pallas_call(
        body,
        out_shape=[jax.ShapeDtypeStruct(shape, jnp.float32) for shape in shapes],
        grid_spec=pltpu.PrefetchScalarGridSpec(
            num_scalar_prefetch=2,
            grid=(1,),
            in_specs=[pl.BlockSpec(memory_space=pltpu.HBM)],
            out_specs=[pl.BlockSpec(shape, lambda *_: (0, 0, 0)) for shape in shapes],
            scratch_shapes=[pltpu.VMEM((total, rows, width), jnp.float32), pltpu.SemaphoreType.DMA((total,))],
        ),
        cost_estimate=pl.CostEstimate(flops=0, bytes_accessed=total * rows * width * 6, transcendentals=0),
        compiler_params=pltpu.CompilerParams(vmem_limit_bytes=KERNEL_VMEM + total * rows * width * 10),
        name="pack",
    )(scalars, order, pltpu.with_memory_space_constraint(array, pltpu.HBM))
    return [outs[3 * number : 3 * number + 3] for number in range(len(groups))]


def unpack(own, near, far, place, core):
    count, rows, quarter = own.shape
    scalars = jnp.stack([place, core]).astype(jnp.int32)

    def body(info, own_ref, near_ref, near_other, far_ref, far_other, out):
        my_place, my_core = info[0], info[1]

        def put(slot, code, value):
            out[slot, pl.ds(pl.multiple_of((my_place ^ code) * rows, rows), rows), :] = value

        for slot in range(2):
            put(slot, 0, own_ref[slot])
            put(slot, 1 + my_core, near_ref[slot])
            put(slot, 2 - my_core, near_other[slot])
            put(slot, 3, jnp.where(my_core == slot, far_ref[0], far_other[0]))

    single = pl.BlockSpec((1, rows, quarter), lambda step, *_: (step, 0, 0))
    double = pl.BlockSpec((2, rows, quarter), lambda step, *_: (step, 0, 0))
    return pl.pallas_call(
        body,
        out_shape=jax.ShapeDtypeStruct((count, 4 * rows, quarter), jnp.float32),
        grid_spec=pltpu.PrefetchScalarGridSpec(
            num_scalar_prefetch=1,
            grid=(count // 2,),
            in_specs=[double, double, double, single, single],
            out_specs=pl.BlockSpec((2, 4 * rows, quarter), lambda step, *_: (step, 0, 0)),
        ),
        cost_estimate=pl.CostEstimate(flops=0, bytes_accessed=count * rows * quarter * 32, transcendentals=0),
        compiler_params=pltpu.CompilerParams(vmem_limit_bytes=KERNEL_VMEM),
        name="unpack",
    )(scalars, own, *near, *far)


def exchange(packed, masks, size, place, core):
    own, near, far = packed
    routes = [(2 * i + c, 2 * (i ^ masks[c]) + c) for i in range(size) for c in range(2)]
    near = lax.ppermute(near, ("blk", "grp"), routes)
    far = swap(far, masks[2], size)
    near_other, far_other = across(near), across(far)
    return unpack(own, (near, near_other), (far, far_other), place, core)


def grid_local(size, schur_blocks, residual, direction, corner_map, panel_order, coarse_factor, block_inverses):
    panels, rows_b, width = block_inverses.shape
    sub_count, corners = corner_map.shape
    vectors = residual.shape[-1]
    half = vectors // 2
    quarter = width // 4
    here = sub_count * corners
    device = lax.axis_index("blk")
    core = lax.axis_index("grp")
    place_i, place_j = device % 4, device // 4
    masks_i, masks_j = (1, 2, 3), (4, 8, 12)

    inverses, coupling, packed = {}, {}, {}
    pairs = [(t, u) for t in range(panels) for u in range(t)]

    def at_step(step, message):
        for kind in ("inv", "low"):
            chosen = [batch for batch in BATCHES if batch[0].startswith(kind) and batch[3] == step]
            if not chosen:
                continue
            if kind == "inv":
                groups = [[(t,) for t in range(low, high)] for _, low, high, *_ in chosen]
                how = (block_inverses, panel_order, groups, place_j, core, put_columns_of_j, message)
            else:
                groups = [pairs[low:high] for _, low, high, *_ in chosen]
                how = (coarse_factor, panel_order, groups, place_i, core, put_columns_of_i, message)
            packed.update(zip([batch[0] for batch in chosen], pack(*how)))
        for name, low, high, packing, sending, _ in BATCHES:
            if sending != step:
                continue
            ready = packed[name]
            if packing != sending:
                ready = [*ready[:1], *after(tuple(ready[1:]), message)]
            if name.startswith("inv"):
                blocks = exchange(ready, masks_j, size, place_j, core)
                inverses.update({low + at: blocks[at] for at in range(high - low)})
            else:
                blocks = exchange(ready, masks_i, size, place_i, core)
                coupling.update({pair: blocks[at] for at, pair in enumerate(pairs[low:high])})

    at_step(None, None)

    applied = jnp.einsum(
        "sij,sjv->siv", schur_blocks, direction.astype(jnp.bfloat16), preferred_element_type=jnp.float32
    )
    sums = jnp.stack(
        [
            jnp.sum(residual * residual, axis=(0, 1)),
            jnp.sum(direction * applied, axis=(0, 1)),
            jnp.sum(residual * applied, axis=(0, 1)),
            jnp.sum(applied * applied, axis=(0, 1)),
        ]
    )
    corner_res = residual[:, :corners, :].reshape(here, vectors)
    corner_app = applied[:, :corners, :].reshape(here, vectors)
    low_half = jnp.concatenate([corner_res[:, :half], corner_app[:, :half]], axis=1)
    high_half = jnp.concatenate([corner_res[:, half:], corner_app[:, half:]], axis=1)
    own_slots = corner_map.reshape(here)
    turn = jnp.sum(
        jnp.where(
            (own_slots // rows_b)[:, None] == panel_order[None, :], jnp.arange(panels, dtype=jnp.int32)[None, :], 0
        ),
        axis=1,
    )
    slots = (turn * rows_b + own_slots % rows_b).reshape(1, here).astype(jnp.float32)
    common = jnp.concatenate([sums, jnp.pad(slots, ((0, 3), (0, vectors - here)))], axis=0)
    keep = jnp.where(core == 0, low_half, high_half)
    give = jnp.where(core == 0, high_half, low_half)
    other = across(jnp.concatenate([give, common], axis=0))
    values = jnp.concatenate([keep, other[:here]], axis=0)
    sums = sums + other[here : here + 4]
    slots = jnp.concatenate([slots, other[here + 4 : here + 5, :here]], axis=1).astype(jnp.int32)[0][:, None]

    columns = lax.broadcasted_iota(jnp.int32, (1, panels * quarter), 1)
    column_slot = columns // quarter * rows_b + columns % rows_b
    column_place = columns % quarter // rows_b
    into = (slots == jnp.where(column_place == place_i, column_slot, -1)).astype(jnp.float32)
    outof = (slots == jnp.where(column_place == place_j, column_slot, -1)).astype(jnp.float32)
    coarse = lax.dot_general(
        values, into, (((0,), (0,)), ((), ())), precision=exact, preferred_element_type=jnp.float32
    )

    pairwise = lax.broadcasted_iota(jnp.int32, (1, 2 * rows_b), 1)
    into_first = slots == jnp.where(pairwise // rows_b == place_i % 2, pairwise % rows_b, -1)
    first = lax.dot_general(
        values,
        into_first.astype(jnp.float32),
        (((0,), (0,)), ((), ())),
        precision=exact,
        preferred_element_type=jnp.float32,
    )
    first = jnp.concatenate([first, jnp.pad(sums, ((0, 4), (0, 0)))], axis=0)
    at_step(0, first)
    parts = parts_over([first] * 3, masks_i, size)
    same, other = first + parts[0], parts[1] + parts[2]
    in_low = place_i // 2 == 0
    with_sums = jnp.concatenate([jnp.where(in_low, same, other), jnp.where(in_low, other, same)], axis=1)
    sums = same[vectors:] + other[vectors:]
    partial = times_transposed(with_sums[:vectors], inverses[0], fine)
    with_sums = jnp.concatenate([partial, jnp.pad(sums, ((0, 0), (0, quarter - vectors)))], axis=0)
    at_step(1, with_sums)
    at_step("1b", with_sums)
    with_sums = total_over(with_sums, masks_j, size)
    norm_now, curvature, crossed, squared = (with_sums[vectors + k, :vectors] for k in range(4))
    step_size = norm_now / curvature
    norm_next = norm_now - step_size * (2.0 * crossed - step_size * squared)
    residual = residual - step_size * applied
    residual, moved = lax.optimization_barrier((residual, residual + norm_next / norm_now * direction))
    step_half = jnp.where(core == 0, step_size[:half], step_size[half:])[:, None]
    solved = [with_sums[:half] - step_half * with_sums[half:vectors]]
    coarse = coarse[:half] - step_half * coarse[half:]

    for t in range(1, panels):
        target = coarse[:, t * quarter : (t + 1) * quarter]
        for u in range(t - 1):
            target = target - times_transposed(solved[u], coupling[t, u], fine)
        target = lax.optimization_barrier(target)
        target = target - times_transposed(solved[t - 1], coupling[t, t - 1], fine)
        at_step(2 * t, target)
        target = total_over(target, masks_i, size)
        partial = times_transposed(target, inverses[t], fine)
        at_step(2 * t + 1, partial)
        if t + 1 < panels:
            solved.append(total_over(partial, masks_j, size))

    halves = partial[:, : 2 * rows_b], partial[:, 2 * rows_b :]
    own_low = place_j // 2 == 0
    mine, others = jnp.where(own_low, halves[0], halves[1]), jnp.where(own_low, halves[1], halves[0])
    parts = parts_over([mine, others, others], masks_j, size)
    last = mine + parts[0] + parts[1] + parts[2]
    last_slot = (panels - 1) * rows_b + pairwise % rows_b
    outof_last = slots == jnp.where(pairwise // rows_b == place_j % 2, last_slot, -1)

    correction = 0.0
    for t in range(panels - 1):
        correction = correction + times_transposed(outof[:, t * quarter : (t + 1) * quarter], solved[t], exact)
    correction = lax.optimization_barrier(correction)
    correction = correction + times_transposed(outof_last.astype(jnp.float32), last, exact)
    other = across(correction[here:])
    correction = jnp.where(
        core == 0,
        jnp.concatenate([correction[:here], other], axis=1),
        jnp.concatenate([other, correction[:here]], axis=1),
    ).reshape(sub_count, corners, vectors)
    return (residual, moved.at[:, :corners, :].add(correction))


def squares(residual):
    return lax.psum(jnp.sum(residual * residual, axis=(0, 1)), ("blk", "grp"))


def solve(coarse, panel_order, coarse_factor, block_inverses):
    panels = coarse.shape[0]
    pending = jnp.zeros_like(coarse)
    solved = jnp.zeros_like(coarse)
    for position in range(panels):
        current = panel_order[position]
        target = lax.dynamic_index_in_dim(coarse - pending, current, 0, keepdims=False)
        inverse = lax.dynamic_index_in_dim(block_inverses, current, 0, keepdims=False)
        block_value = jnp.dot(
            inverse,
            lax.all_gather(target, "blk", axis=0, tiled=True),
            precision=exact,
            preferred_element_type=jnp.float32,
        )
        solved = lax.dynamic_update_index_in_dim(solved, block_value, current, 0)
        if position + 1 < panels:
            coupling = lax.dynamic_index_in_dim(coarse_factor, current, 1, keepdims=False)
            pending = pending + jnp.einsum(
                "aic,cv->aiv", coupling, lax.all_gather(block_value, "blk", axis=0, tiled=True), precision=exact
            )
    return solved


def row_local(schur_blocks, residual, direction, corner_map, panel_order, coarse_factor, block_inverses):
    panels, rows_b = block_inverses.shape[:2]
    sub_count, corners = corner_map.shape
    columns_iota = lax.broadcasted_iota(jnp.int32, (sub_count, corners, panels * rows_b), 2)
    placing = (corner_map[:, :, None] == columns_iota).astype(jnp.float32)
    norm_now = squares(residual)
    applied = jnp.einsum(
        "sij,sjv->siv", schur_blocks, direction.astype(jnp.bfloat16), preferred_element_type=jnp.float32
    )
    curvature = lax.psum(jnp.sum(direction * applied, axis=(0, 1)), ("blk", "grp"))
    residual = residual - norm_now / curvature * applied
    norm_next = squares(residual)
    corner_part = jnp.einsum("scm,scv->mv", placing, residual[:, :corners, :], precision=exact)
    coarse_part = lax.psum(corner_part.reshape(panels, rows_b, -1), "grp")
    solved = solve(coarse_part, panel_order, coarse_factor, block_inverses)
    correction = jnp.einsum("scm,mv->scv", placing, solved.reshape(panels * rows_b, -1), precision=exact)
    direction = (residual + norm_next / norm_now * direction).at[:, :corners, :].add(correction)
    return (residual, direction)


def solution(mesh):
    in_specs = (
        P(("blk", "grp"), None, None),
        P(("blk", "grp"), None, None),
        P(("blk", "grp"), None, None),
        P(("blk", "grp"), None),
        P(),
        P(None, None, "blk", None),
        P(None, "blk", None),
    )
    out_specs = (P(("blk", "grp"), None, None), P(("blk", "grp"), None, None))
    size = mesh.shape["blk"]

    def local(*args):
        rows_b, _ = args[-1].shape[1:]
        panels, corners = args[-1].shape[0], args[3].shape[0] * args[3].shape[1]
        as_grid = (
            size == 16
            and mesh.shape["grp"] == 2
            and 2 * rows_b == LANES
            and panels % 2 == 0
            and args[1].shape[-1] == LANES
            and corners % 8 == 0
            and corners <= LANES
        )
        return grid_local(size, *args) if as_grid else row_local(*args)

    return jax.shard_map(local, mesh=mesh, in_specs=in_specs, out_specs=out_specs, check_vma=False)
```
